512 devices in a mesh: rep: 4 (over x), exp: 128 (over z, y, core).
Axes of the slice: x: 4, y: 8, z: 8, core: 2. Of those that a mesh axis runs over, the one named last changes fastest.
Arguments:
- tokens: bfloat16 [3072, 2048], P('exp', 'rep'), may hold values from -6 to 6
- cotangent: bfloat16 [3072, 2048], P('exp', 'rep'), may hold values from -6 to 6
- router_weight: bfloat16 [3072, 8], P('exp'), may hold values from 0.019897461 to 0.5
- expert_ids: int32 [3072, 8], P('exp'), may hold values from 0 to 127, all different within a row; in each aligned block of 24 rows (0 to 23, 24 to 47, ...) at most 2 rows name the same one
- w_gate: bfloat16 [128, 2048, 768], P('exp', 'rep'), may hold values from -0.125 to 0.125
- w_up: bfloat16 [128, 2048, 768], P('exp', 'rep'), may hold values from -0.125 to 0.125
- w_down: bfloat16 [128, 768, 2048], P('exp', None, 'rep'), may hold values from -0.21875 to 0.21875
Outputs:
- mixed: bfloat16 [3072, 2048], P('exp', 'rep')
- token_grad: bfloat16 [3072, 2048], P('exp', 'rep')
- router_grad: bfloat16 [3072, 8], P('exp')
- gate_weight_grad: bfloat16 [128, 2048, 768], P('exp', 'rep')
- up_weight_grad: bfloat16 [128, 2048, 768], P('exp', 'rep')
- down_weight_grad: bfloat16 [128, 768, 2048], P('exp', None, 'rep')
The draws below stay inside these ranges and needn't reach their ends.
Inputs may be any that keep to these rules, and one draw needn't show every extreme that they name: `expert_ids`: each row names 8 different experts. Among the 24 rows of one index of exp (aligned blocks) no expert is named more than 2 times, a bound that some block reaches.
All inputs are finite; a program needn't handle non-finite values.
Results may differ from the reference program's by a relative error of at most 0.013.
Values may be sent and summed in bfloat16 or wider, within the bound.
No kernel may reach another device: no remote copies, remote signals or barrier semaphores. Data moves between devices by JAX's collectives and lax.ppermute only.
A program may use at most 64 MiB of HBM per device.

```python
import math
import jax
import jax.numpy as jnp
import numpy as np
from jax import lax

D = 2048
FF = 768
TOK_DEV = 24
EXPERTS = 128
TOP = 8
CAP = 2
TOKENS = 3072
N_EXP = 128


def level_of(rng, shape, pieces, low, top_value):
    def one(axis_at, blocks):
        draws = jax.random.uniform(jax.random.fold_in(jax.random.fold_in(rng, 6), axis_at), (blocks,), jnp.float32, low / len(pieces), top_value / len(pieces))
        return jnp.repeat(jnp.exp(draws), shape[axis_at] // blocks).reshape((-1,) + (1,) * (len(shape) - axis_at - 1))

    loudness = one(*pieces[0])
    for cut in pieces[1:]:
        loudness = loudness * one(*cut)
    return loudness


def routed_block(key, own, number, rows, count, top, bound, skew):
    order = jax.random.permutation(key, count)
    heavy_load, usual = shares(count, rows * top, bound, skew, True), shares(count, rows * top, bound, skew, False)
    places = jnp.arange(count)

    def named(lengths, offset_by):
        used = int((lengths > 0).sum())
        fixed = max(1, used // 4)
        passed = fixed + (places - fixed + offset_by * (used - fixed)) % max(1, count - fixed)
        return jnp.zeros((count,), jnp.int32).at[order[jnp.where(places < fixed, places, passed)]].set(jnp.asarray(lengths, jnp.int32))

    lengths = jnp.where(number % 4 == 0, named(heavy_load, number // 4), named(usual, number - number // 4 - 1))
    mixed = jax.random.permutation(jax.random.fold_in(own, 3), count)
    source_of, sink = mixed[0:count // 2 * 2:2], mixed[1:count // 2 * 2:2]
    slack = jnp.minimum(lengths[source_of] - 1, bound - lengths[sink]) // 2
    slack = jnp.where((source_of == order[0]) | (sink == order[0]) | (lengths[sink] == 0), 0, jnp.maximum(slack, 0))
    passed = jax.random.randint(jax.random.fold_in(own, 4), (count // 2,), 0, 1 << 20) % (slack + 1)
    lengths = lengths.at[source_of].add(-passed).at[sink].add(passed)
    members = jnp.searchsorted(jnp.cumsum(lengths), jnp.arange(rows * top), side="right").astype(jnp.int32)
    grid = members.reshape(top, rows).T
    grid = grid[jax.random.permutation(jax.random.fold_in(own, 1), rows)]
    offset_by = jax.random.randint(jax.random.fold_in(own, 2), (rows, 1), 0, top)
    return jnp.take_along_axis(grid, (jnp.arange(top)[None, :] + offset_by) % top, axis=1)


def shares(amount, total, most, lean, full):
    portions = [(1 << 20) // math.isqrt(rank ** lean) + 1 for rank in range(1, amount + 1)]
    largest = most if full else min(most, max(-(-total // amount), total * portions[0] // sum(portions)))
    least = 1 if total - largest >= amount - 1 else 0
    holding, rest = [largest] + [least] * (amount - 1), total - largest - least * (amount - 1)
    while rest > 0:
        candidates = [i for i in range(1, amount) if holding[i] < largest] or [i for i in range(1, amount) if holding[i] < most]
        pool, remaining = sum([portions[i] for i in candidates]), rest
        for i in candidates:
            more = min(most - holding[i], max(1, remaining * portions[i] // pool), rest)
            holding[i] = holding[i] + more
            rest = rest - more
    return np.array(holding)


def normal_values(stream_key, extent, deviation, most, shards=(), held_as=jnp.bfloat16):
    array = deviation * jax.random.normal(stream_key, extent, jnp.float32)
    if shards:
        array = array * level_of(stream_key, extent, shards, -0.22, 0.18)
    return jnp.clip(array, -most, most).astype(held_as)


def setup_inputs(seed: int = 0) -> dict:
    splits = jax.random.split(jax.random.key(seed), 8)
    tokens = normal_values(splits[0], (TOKENS, D), 1.0, 6.0, ((0, 128), (1, 4)))
    cotangent = normal_values(splits[1], (TOKENS, D), 1.0, 6.0, ((0, 128), (1, 4)))
    router_weight = jnp.clip(jnp.exp(math.log(0.5) - 3.224016 * jax.random.uniform(splits[2], (TOKENS, TOP), jnp.float32) ** level_of(splits[2], (TOKENS, TOP), ((0, 128),), -0.2, 0.2)), 0.019897461, 0.5).astype(jnp.bfloat16)
    expert_ids_keys = jax.random.split(jax.random.fold_in(splits[3], 1), TOKENS // TOK_DEV)
    expert_ids_turns = jax.random.permutation(jax.random.fold_in(splits[3], 3), TOKENS // TOK_DEV)
    expert_ids = jax.vmap(lambda own, number: routed_block(jax.random.fold_in(splits[3], 2), own, number, TOK_DEV, EXPERTS, TOP, CAP, 2))(expert_ids_keys, expert_ids_turns).reshape((TOKENS, TOP))
    w_gate = normal_values(splits[4], (EXPERTS, D, FF), D ** -0.5, 0.125, ((0, 128), (1, 4)))
    w_up = normal_values(splits[5], (EXPERTS, D, FF), D ** -0.5, 0.125, ((0, 128), (1, 4)))
    w_down = normal_values(splits[6], (EXPERTS, FF, D), FF ** -0.5, 0.21875, ((0, 128), (2, 4)))
    return {"tokens": tokens, "cotangent": cotangent, "router_weight": router_weight, "expert_ids": expert_ids, "w_gate": w_gate, "w_up": w_up, "w_down": w_down}


def slot_layout(expert_ids):
    token_count = expert_ids.shape[0]
    expert_range = jnp.arange(EXPERTS, dtype=jnp.int32)
    per_token = jnp.sum((expert_ids[:, :, None] == expert_range[None, None, :]).astype(jnp.int32), axis=1)
    blocked = per_token.reshape(N_EXP, TOK_DEV, EXPERTS)
    earlier = (jnp.cumsum(blocked, axis=1) - blocked).reshape(token_count, EXPERTS)
    ranking = jnp.take_along_axis(earlier, expert_ids, axis=1).astype(jnp.int32)
    source = (jnp.arange(token_count, dtype=jnp.int32) // TOK_DEV).astype(jnp.int32)
    return (source[:, None] * CAP + ranking).astype(jnp.int32)


def expert_pass(tokens, cotangent, table_rows, table_weights, gate_mat, up_mat, down_mat):
    valid = table_rows >= 0
    safe_rows = jnp.maximum(table_rows, 0).astype(jnp.int32)
    inputs = jnp.where(valid[:, None], tokens[safe_rows], jnp.zeros((), tokens.dtype))
    upstream = jnp.where(valid[:, None], cotangent[safe_rows], jnp.zeros((), cotangent.dtype))
    gate = jnp.dot(inputs, gate_mat, preferred_element_type=jnp.float32)
    upval = jnp.dot(inputs, up_mat, preferred_element_type=jnp.float32)
    active = jax.nn.silu(gate)
    hidden = (active * upval).astype(jnp.bfloat16)
    outputs = jnp.dot(hidden, down_mat, preferred_element_type=jnp.float32).astype(jnp.bfloat16)
    out_delta = (table_weights[:, None] * upstream.astype(jnp.float32)).astype(jnp.bfloat16)
    hidden_delta = jnp.dot(out_delta, down_mat.T, preferred_element_type=jnp.float32)
    sigmoid = jax.nn.sigmoid(gate)
    gate_delta = (hidden_delta * upval * sigmoid * (1.0 + gate * (1.0 - sigmoid))).astype(jnp.bfloat16)
    up_delta = (hidden_delta * active).astype(jnp.bfloat16)
    down_grad = jnp.dot(hidden.T, out_delta, preferred_element_type=jnp.float32).astype(jnp.bfloat16)
    gate_grad = jnp.dot(inputs.T, gate_delta, preferred_element_type=jnp.float32).astype(jnp.bfloat16)
    up_grad = jnp.dot(inputs.T, up_delta, preferred_element_type=jnp.float32).astype(jnp.bfloat16)
    token_delta = (jnp.dot(gate_delta, gate_mat.T, preferred_element_type=jnp.float32)
                   + jnp.dot(up_delta, up_mat.T, preferred_element_type=jnp.float32)).astype(jnp.bfloat16)
    return outputs, token_delta, gate_grad, up_grad, down_grad


def reference(tokens, cotangent, router_weight, expert_ids, w_gate, w_up, w_down):
    token_count = tokens.shape[0]
    slot_pos = slot_layout(expert_ids)
    token_index = jnp.broadcast_to(jnp.arange(token_count, dtype=jnp.int32)[:, None], expert_ids.shape)
    table = jnp.full((EXPERTS, N_EXP * CAP), -1, jnp.int32).at[expert_ids, slot_pos].set(token_index)
    weight_table = jnp.zeros((EXPERTS, N_EXP * CAP), jnp.float32).at[expert_ids, slot_pos].set(
        router_weight.astype(jnp.float32))

    def one_expert(packed):
        table_rows, table_weights, gate_mat, up_mat, down_mat = packed
        return expert_pass(tokens, cotangent, table_rows, table_weights, gate_mat, up_mat, down_mat)

    outputs, token_delta, gate_grad, up_grad, down_grad = lax.map(
        one_expert, (table, weight_table, w_gate, w_up, w_down))
    route_out = outputs[expert_ids, slot_pos].astype(jnp.float32)
    route_delta = token_delta[expert_ids, slot_pos].astype(jnp.float32)
    weights = router_weight.astype(jnp.float32)
    mixed = jnp.sum(weights[:, :, None] * route_out, axis=1).astype(jnp.bfloat16)
    router_grad = jnp.sum(route_out * cotangent.astype(jnp.float32)[:, None, :], axis=2).astype(jnp.bfloat16)
    token_grad = jnp.sum(route_delta, axis=1).astype(jnp.bfloat16)
    return mixed, token_grad, router_grad, gate_grad, up_grad, down_grad
```

```python
import jax
import jax.numpy as jnp
from jax import lax
from jax.sharding import PartitionSpec as P

BF = jnp.bfloat16
F32 = jnp.float32
LANES = 128


def mm(a, b, dims=(((1,), (0,)), ((), ()))):
    return lax.dot_general(a, b, dims, preferred_element_type=F32)


NT = (((1,), (1,)), ((), ()))
TN = (((0,), (0,)), ((), ()))


def swap(x, axis):
    return lax.all_to_all(x, axis, split_axis=0, concat_axis=0, tiled=True)


def slot_tables(expert_ids, router_weight, experts, capacity):
    rows = expert_ids.shape[0]
    match = expert_ids[:, :, None] == jnp.arange(experts, dtype=jnp.int32)[None, None, :]
    named = jnp.sum(match.astype(F32), axis=1)
    weight = jnp.sum(jnp.where(match, router_weight.astype(F32)[:, :, None], 0.0), axis=1)
    row = jnp.arange(rows)
    before = (row[None, :] < row[:, None]).astype(BF)
    earlier = mm(before, named.astype(BF))
    slot = jnp.arange(capacity, dtype=F32)
    here = (earlier[:, :, None] == slot) & (named[:, :, None] > 0)
    placing = here.astype(BF).reshape(rows, experts * capacity)
    weighting = jnp.where(here, weight[:, :, None], 0.0).astype(BF)
    return match, placing, weighting.reshape(rows, experts * capacity)


def local(tokens, cotangent, router_weight, expert_ids, w_gate, w_up, w_down):
    experts = lax.axis_size("exp")
    reps = lax.axis_size("rep")
    rows, top = expert_ids.shape
    capacity = min(rows, max(2, rows * top * 3 // (2 * experts)))
    width = tokens.shape[1]
    hid = w_gate.shape[2]
    total = experts * capacity
    part = total // reps
    gate_mat, up_mat, down_mat = w_gate[0], w_up[0], w_down[0]

    match, placing, weighting = slot_tables(expert_ids, router_weight, experts, capacity)
    sent = jnp.concatenate(
        [mm(placing, tokens, TN).astype(BF), mm(weighting, cotangent, TN).astype(BF)], axis=1
    )
    recv = swap(sent.reshape(experts, capacity, 2 * width), "exp").reshape(total, 2 * width)
    inputs, out_delta = recv[:, :width], recv[:, width:]

    partial = jnp.concatenate(
        [
            mm(inputs, gate_mat).astype(BF),
            mm(inputs, up_mat).astype(BF),
            mm(out_delta, down_mat, NT).astype(BF),
        ],
        axis=1,
    )
    pieces = swap(partial.reshape(reps, part, 3 * hid), "rep")
    summed = jnp.sum(pieces.astype(F32), axis=0)
    gate, upval, hidden_delta = summed[:, :hid], summed[:, hid : 2 * hid], summed[:, 2 * hid :]
    sigmoid = 1.0 / (1.0 + jnp.exp(-gate))
    active = gate * sigmoid
    hidden = (active * upval).astype(BF)
    gate_delta = (hidden_delta * upval * sigmoid * (1.0 + gate * (1.0 - sigmoid))).astype(BF)
    up_delta = (hidden_delta * active).astype(BF)
    scaled = jnp.sum(hidden.astype(F32) * hidden_delta, axis=1, keepdims=True).astype(BF)
    mine = jnp.concatenate(
        [hidden, gate_delta, up_delta, jnp.broadcast_to(scaled, (part, LANES))], axis=1
    )
    full = swap(jnp.broadcast_to(mine[None], (reps,) + mine.shape), "rep").reshape(total, -1)
    hidden, gate_delta = full[:, :hid], full[:, hid : 2 * hid]
    up_delta, scaled = full[:, 2 * hid : 3 * hid], full[:, 3 * hid :]

    outputs = mm(hidden, down_mat).astype(BF)
    token_delta = (mm(gate_delta, gate_mat, NT) + mm(up_delta, up_mat, NT)).astype(BF)
    back = jnp.concatenate([outputs, token_delta, scaled], axis=1)
    back = swap(back.reshape(experts, capacity, back.shape[1]), "exp").reshape(total, -1)

    down_grad = mm(hidden, out_delta, TN).astype(BF)
    gate_grad = mm(inputs, gate_delta, TN).astype(BF)
    up_grad = mm(inputs, up_delta, TN).astype(BF)

    mixed = mm(weighting, back[:, :width]).astype(BF)
    token_grad = mm(placing, back[:, width : 2 * width]).astype(BF)
    routed = back[:, 2 * width].astype(F32).reshape(1, experts, capacity)
    by_expert = jnp.sum(placing.astype(F32).reshape(rows, experts, capacity) * routed, axis=2)
    router_grad = jnp.sum(jnp.where(match, by_expert[:, None, :], 0.0), axis=2)
    router_grad = (router_grad / router_weight.astype(F32)).astype(BF)
    return (mixed, token_grad, router_grad, gate_grad[None], up_grad[None], down_grad[None])


def solution(mesh):
    return jax.shard_map(
        local,
        mesh=mesh,
        in_specs=(
            P("exp", "rep"),
            P("exp", "rep"),
            P("exp", None),
            P("exp", None),
            P("exp", "rep", None),
            P("exp", "rep", None),
            P("exp", None, "rep"),
        ),
        out_specs=(
            P("exp", "rep"),
            P("exp", "rep"),
            P("exp", None),
            P("exp", "rep", None),
            P("exp", "rep", None),
            P("exp", None, "rep"),
        ),
        check_vma=False,
    )
```

```python
import jax
import jax.numpy as jnp
from jax import lax
from jax.sharding import PartitionSpec as P

BF = jnp.bfloat16
F32 = jnp.float32
LANES = 128


def mm(a, b, dims=(((1,), (0,)), ((), ()))):
    return lax.dot_general(a, b, dims, preferred_element_type=F32)


NT = (((1,), (1,)), ((), ()))
TN = (((0,), (0,)), ((), ()))


def swap(x, axis):
    return lax.all_to_all(x, axis, split_axis=0, concat_axis=0, tiled=True)


def slot_tables(expert_ids, router_weight, experts, capacity):
    rows = expert_ids.shape[0]
    match = expert_ids[:, :, None] == jnp.arange(experts, dtype=jnp.int32)[None, None, :]
    named = jnp.sum(match.astype(F32), axis=1)
    weight = jnp.sum(jnp.where(match, router_weight.astype(F32)[:, :, None], 0.0), axis=1)
    row = jnp.arange(rows)
    before = (row[None, :] < row[:, None]).astype(BF)
    earlier = mm(before, named.astype(BF))
    slot = jnp.arange(capacity, dtype=F32)
    here = (earlier[:, :, None] == slot) & (named[:, :, None] > 0)
    placing = here.astype(BF).reshape(rows, experts * capacity)
    weighting = jnp.where(here, weight[:, :, None], 0.0).astype(BF)
    return match, placing, weighting.reshape(rows, experts * capacity)


def local(tokens, cotangent, router_weight, expert_ids, w_gate, w_up, w_down):
    experts = lax.axis_size("exp")
    reps = lax.axis_size("rep")
    rows, top = expert_ids.shape
    capacity = min(rows, max(2, rows * top * 3 // (2 * experts)))
    width = tokens.shape[1]
    hid = w_gate.shape[2]
    total = experts * capacity
    part = total // reps
    gate_mat, up_mat, down_mat = w_gate[0], w_up[0], w_down[0]

    match, placing, weighting = slot_tables(expert_ids, router_weight, experts, capacity)
    sent = jnp.concatenate(
        [mm(placing, tokens, TN).astype(BF), mm(weighting, cotangent, TN).astype(BF)], axis=1
    )
    recv = swap(sent.reshape(experts, capacity, 2 * width), "exp").reshape(total, 2 * width)

    me = lax.axis_index("rep")

    def rows_of(array, owner):
        return lax.dynamic_slice_in_dim(array, owner * part, part, 0)

    def to_peer(array, step):
        return lax.ppermute(array, "rep", [(i, (i + step) % reps) for i in range(reps)])

    def partial(owner):
        rows_in = rows_of(recv, owner)
        return jnp.concatenate(
            [
                mm(rows_in[:, :width], gate_mat),
                mm(rows_in[:, :width], up_mat),
                mm(rows_in[:, width:], down_mat, NT),
            ],
            axis=1,
        )

    steps = [2, 1, 3]
    arrived = [to_peer(partial((me + d) % reps).astype(BF), d) for d in steps]
    summed = partial(me)
    for piece in arrived:
        summed = summed + piece.astype(F32)
    gate, upval, hidden_delta = summed[:, :hid], summed[:, hid : 2 * hid], summed[:, 2 * hid :]
    sigmoid = 1.0 / (1.0 + jnp.exp(-gate))
    active = gate * sigmoid
    hidden = (active * upval).astype(BF)
    gate_delta = (hidden_delta * upval * sigmoid * (1.0 + gate * (1.0 - sigmoid))).astype(BF)
    up_delta = (hidden_delta * active).astype(BF)
    scaled = jnp.sum(hidden.astype(F32) * hidden_delta, axis=1, keepdims=True).astype(BF)
    mine = jnp.concatenate(
        [hidden, gate_delta, up_delta, jnp.broadcast_to(scaled, (part, LANES))], axis=1
    )
    owners = [me] + [(me - d) % reps for d in steps]
    pieces = [mine] + [to_peer(mine, d) for d in steps]

    back = jnp.zeros((experts, capacity, 2 * width + LANES), BF)
    for owner, piece in zip(owners, pieces):
        outputs = mm(piece[:, :hid], down_mat).astype(BF)
        token_delta = mm(piece[:, hid : 2 * hid], gate_mat, NT)
        token_delta = (token_delta + mm(piece[:, 2 * hid : 3 * hid], up_mat, NT)).astype(BF)
        block = jnp.concatenate([outputs, token_delta, piece[:, 3 * hid :]], axis=1)
        block = block.reshape(part // capacity, capacity, 2 * width + LANES)
        back = lax.dynamic_update_slice_in_dim(back, block, owner * (part // capacity), 0)
    back = swap(back, "exp").reshape(total, -1)

    full = jnp.concatenate(pieces, axis=0)
    recv = jnp.concatenate([rows_of(recv, owner) for owner in owners], axis=0)
    inputs, out_delta = recv[:, :width], recv[:, width:]
    down_grad = mm(full[:, :hid], out_delta, TN).astype(BF)
    gate_grad = mm(inputs, full[:, hid : 2 * hid], TN).astype(BF)
    up_grad = mm(inputs, full[:, 2 * hid : 3 * hid], TN).astype(BF)

    mixed = mm(weighting, back[:, :width]).astype(BF)
    token_grad = mm(placing, back[:, width : 2 * width]).astype(BF)
    routed = back[:, 2 * width].astype(F32).reshape(1, experts, capacity)
    by_expert = jnp.sum(placing.astype(F32).reshape(rows, experts, capacity) * routed, axis=2)
    router_grad = jnp.sum(jnp.where(match, by_expert[:, None, :], 0.0), axis=2)
    router_grad = (router_grad / router_weight.astype(F32)).astype(BF)
    return (mixed, token_grad, router_grad, gate_grad[None], up_grad[None], down_grad[None])


def solution(mesh):
    return jax.shard_map(
        local,
        mesh=mesh,
        in_specs=(
            P("exp", "rep"),
            P("exp", "rep"),
            P("exp", None),
            P("exp", None),
            P("exp", "rep", None),
            P("exp", "rep", None),
            P("exp", None, "rep"),
        ),
        out_specs=(
            P("exp", "rep"),
            P("exp", "rep"),
            P("exp", None),
            P("exp", "rep", None),
            P("exp", "rep", None),
            P("exp", None, "rep"),
        ),
        check_vma=False,
    )
```

```python
import jax
import jax.numpy as jnp
from jax import lax
from jax.sharding import PartitionSpec as P

BF = jnp.bfloat16
F32 = jnp.float32
LANES = 128


def mm(a, b, dims=(((1,), (0,)), ((), ()))):
    return lax.dot_general(a, b, dims, preferred_element_type=F32)


NT = (((1,), (1,)), ((), ()))
TN = (((0,), (0,)), ((), ()))


def swap(x, axis):
    return lax.all_to_all(x, axis, split_axis=0, concat_axis=0, tiled=True)


def slot_tables(ids, weight, experts, capacity):
    rows = ids.shape[1]
    slot = jnp.arange(experts * capacity, dtype=jnp.int32)[:, None]
    match = ids[:, None, :] == (slot // capacity)[None]
    named = jnp.sum(match.astype(F32), axis=0)
    share = jnp.sum(jnp.where(match, weight[:, None, :], 0.0), axis=0)
    row = jnp.arange(rows)
    before = (row[:, None] < row[None, :]).astype(BF)
    earlier = mm(named.astype(BF), before)
    here = (named > 0) & (earlier == (slot % capacity).astype(F32))
    return match, here, jnp.where(here, share, 0.0).astype(BF)


def local(tokens, cotangent, router_weight, expert_ids, w_gate, w_up, w_down):
    experts = lax.axis_size("exp")
    reps = lax.axis_size("rep")
    rows, top = expert_ids.shape
    capacity = min(rows, max(2, rows * top * 3 // (2 * experts)))
    width = tokens.shape[1]
    hid = w_gate.shape[2]
    total = experts * capacity
    part = total // reps
    gate_mat, up_mat, down_mat = w_gate[0], w_up[0], w_down[0]

    weight = router_weight.T.astype(F32)
    match, here, weighting = slot_tables(expert_ids.T, weight, experts, capacity)
    placing = here.astype(BF)
    sent = jnp.concatenate(
        [mm(placing, tokens).astype(BF), mm(weighting, cotangent).astype(BF)], axis=1
    )
    recv = swap(sent.reshape(experts, capacity, 2 * width), "exp").reshape(total, 2 * width)
    inputs, out_delta = recv[:, :width], recv[:, width:]

    partial = jnp.concatenate(
        [
            mm(inputs, gate_mat).astype(BF),
            mm(inputs, up_mat).astype(BF),
            mm(out_delta, down_mat, NT).astype(BF),
        ],
        axis=1,
    )
    pieces = swap(partial.reshape(reps, part, 3 * hid), "rep")
    summed = jnp.sum(pieces.astype(F32), axis=0)
    gate, upval, hidden_delta = summed[:, :hid], summed[:, hid : 2 * hid], summed[:, 2 * hid :]
    sigmoid = 1.0 / (1.0 + jnp.exp(-gate))
    active = gate * sigmoid
    hidden = (active * upval).astype(BF)
    gate_delta = (hidden_delta * upval * sigmoid * (1.0 + gate * (1.0 - sigmoid))).astype(BF)
    up_delta = (hidden_delta * active).astype(BF)
    scaled = jnp.sum(hidden.astype(F32) * hidden_delta, axis=1, keepdims=True).astype(BF)
    mine = jnp.concatenate(
        [hidden, gate_delta, up_delta, jnp.broadcast_to(scaled, (part, LANES))], axis=1
    )
    full = swap(jnp.broadcast_to(mine[None], (reps,) + mine.shape), "rep").reshape(total, -1)
    hidden, gate_delta = full[:, :hid], full[:, hid : 2 * hid]
    up_delta, scaled = full[:, 2 * hid : 3 * hid], full[:, 3 * hid :]

    outputs = mm(hidden, down_mat).astype(BF)
    token_delta = (mm(gate_delta, gate_mat, NT) + mm(up_delta, up_mat, NT)).astype(BF)
    back = jnp.concatenate([outputs, token_delta, scaled], axis=1)
    back = swap(back.reshape(experts, capacity, back.shape[1]), "exp").reshape(total, -1)

    down_grad = mm(hidden, out_delta, TN).astype(BF)
    gate_grad = mm(inputs, gate_delta, TN).astype(BF)
    up_grad = mm(inputs, up_delta, TN).astype(BF)

    mixed = mm(weighting, back[:, :width], TN).astype(BF)
    token_grad = mm(placing, back[:, width : 2 * width], TN).astype(BF)
    routed = jnp.where(here, back[:, 2 * width :][:, :1].astype(F32), 0.0)
    router_grad = jnp.sum(jnp.where(match, routed[None], 0.0), axis=1)
    router_grad = (router_grad / weight).astype(BF).T
    return (mixed, token_grad, router_grad, gate_grad[None], up_grad[None], down_grad[None])


def solution(mesh):
    return jax.shard_map(
        local,
        mesh=mesh,
        in_specs=(
            P("exp", "rep"),
            P("exp", "rep"),
            P("exp", None),
            P("exp", None),
            P("exp", "rep", None),
            P("exp", "rep", None),
            P("exp", None, "rep"),
        ),
        out_specs=(
            P("exp", "rep"),
            P("exp", "rep"),
            P("exp", None),
            P("exp", "rep", None),
            P("exp", "rep", None),
            P("exp", None, "rep"),
        ),
        check_vma=False,
    )
```

```python
import functools

import jax
import jax.numpy as jnp
from jax import lax
from jax.experimental import pallas as pl
from jax.experimental.pallas import tpu as pltpu
from jax.sharding import PartitionSpec as P

BF = jnp.bfloat16
F32 = jnp.float32
LANES = 128


def mm(a, b, dims=(((1,), (0,)), ((), ()))):
    return lax.dot_general(a, b, dims, preferred_element_type=F32)


NT = (((1,), (1,)), ((), ()))
TN = (((0,), (0,)), ((), ()))


def swap(x, axis):
    return lax.all_to_all(x, axis, split_axis=0, concat_axis=0, tiled=True)


def place_kernel(capacity, ids_ref, weight_ref, tokens_ref, cot_ref, sent_ref, placing_ref, weighting_ref):
    top, rows = ids_ref.shape
    experts = sent_ref.shape[0]
    total = experts * capacity
    width = sent_ref.shape[2] // 2
    slot = lax.broadcasted_iota(jnp.int32, (total, rows), 0)
    expert = slot // capacity
    named = jnp.zeros((total, rows), F32)
    share = jnp.zeros((total, rows), F32)
    for k in range(top):
        hit = ids_ref[k : k + 1, :] == expert
        named = named + jnp.where(hit, 1.0, 0.0)
        share = share + jnp.where(hit, weight_ref[k : k + 1, :].astype(F32), 0.0)
    first = lax.broadcasted_iota(jnp.int32, (rows, rows), 0)
    second = lax.broadcasted_iota(jnp.int32, (rows, rows), 1)
    before = jnp.where(first < second, 1.0, 0.0).astype(BF)
    earlier = mm(named.astype(BF), before)
    here = (named > 0.0) & (earlier == (slot % capacity).astype(F32))
    placing = jnp.where(here, 1.0, 0.0).astype(BF)
    weighting = jnp.where(here, share, 0.0).astype(BF)
    placing_ref[...] = placing
    weighting_ref[...] = weighting
    shape = (experts, capacity, width)
    sent_ref[:, :, :width] = mm(placing, tokens_ref[...]).astype(BF).reshape(shape)
    sent_ref[:, :, width:] = mm(weighting, cot_ref[...]).astype(BF).reshape(shape)


def combine_kernel(
    capacity, ids_ref, weight_ref, placing_ref, weighting_ref, back_ref, mixed_ref, grad_ref, router_ref
):
    top, rows = ids_ref.shape
    total = placing_ref.shape[0]
    width = mixed_ref.shape[1]
    mixed_ref[...] = mm(weighting_ref[...], back_ref[:, :width], TN).astype(BF)
    grad_ref[...] = mm(placing_ref[...], back_ref[:, width : 2 * width], TN).astype(BF)
    expert = lax.broadcasted_iota(jnp.int32, (total, rows), 0) // capacity
    routed = back_ref[:, 2 * width :].astype(F32)[:, :rows] * placing_ref[...].astype(F32)
    sums = [
        jnp.sum(jnp.where(ids_ref[k : k + 1, :] == expert, routed, 0.0), axis=0, keepdims=True)
        for k in range(top)
    ]
    sums = jnp.concatenate(sums, axis=0) / weight_ref[...].astype(F32)
    router_ref[...] = sums.astype(BF)


def local(tokens, cotangent, router_weight, expert_ids, w_gate, w_up, w_down):
    experts = lax.axis_size("exp")
    reps = lax.axis_size("rep")
    rows, top = expert_ids.shape
    capacity = min(rows, max(2, rows * top * 3 // (2 * experts)))
    width = tokens.shape[1]
    hid = w_gate.shape[2]
    total = experts * capacity
    part = total // reps
    gate_mat, up_mat, down_mat = w_gate[0], w_up[0], w_down[0]

    ids, weight = expert_ids.T, router_weight.T
    sent, placing, weighting = pl.pallas_call(
        functools.partial(place_kernel, capacity),
        out_shape=(
            jax.ShapeDtypeStruct((experts, capacity, 2 * width), BF),
            jax.ShapeDtypeStruct((total, rows), BF),
            jax.ShapeDtypeStruct((total, rows), BF),
        ),
        name="place",
        in_specs=[pl.BlockSpec(memory_space=pltpu.VMEM)] * 4,
        out_specs=(pl.BlockSpec(memory_space=pltpu.VMEM),) * 3,
        compiler_params=pltpu.CompilerParams(vmem_limit_bytes=6 * 1024 * 1024),
    )(ids, weight, tokens, cotangent)
    recv = swap(sent, "exp").reshape(total, 2 * width)
    inputs, out_delta = recv[:, :width], recv[:, width:]

    partial = jnp.concatenate(
        [
            mm(inputs, gate_mat).astype(BF),
            mm(inputs, up_mat).astype(BF),
            mm(out_delta, down_mat, NT).astype(BF),
        ],
        axis=1,
    )
    pieces = swap(partial.reshape(reps, part, 3 * hid), "rep")
    summed = jnp.sum(pieces.astype(F32), axis=0)
    gate, upval, hidden_delta = summed[:, :hid], summed[:, hid : 2 * hid], summed[:, 2 * hid :]
    sigmoid = 1.0 / (1.0 + jnp.exp(-gate))
    active = gate * sigmoid
    hidden = (active * upval).astype(BF)
    gate_delta = (hidden_delta * upval * sigmoid * (1.0 + gate * (1.0 - sigmoid))).astype(BF)
    up_delta = (hidden_delta * active).astype(BF)
    scaled = jnp.sum(hidden.astype(F32) * hidden_delta, axis=1, keepdims=True).astype(BF)
    mine = jnp.concatenate(
        [hidden, gate_delta, up_delta, jnp.broadcast_to(scaled, (part, LANES))], axis=1
    )
    full = swap(jnp.broadcast_to(mine[None], (reps,) + mine.shape), "rep").reshape(total, -1)
    hidden, gate_delta = full[:, :hid], full[:, hid : 2 * hid]
    up_delta, scaled = full[:, 2 * hid : 3 * hid], full[:, 3 * hid :]

    outputs = mm(hidden, down_mat).astype(BF)
    token_delta = (mm(gate_delta, gate_mat, NT) + mm(up_delta, up_mat, NT)).astype(BF)
    back = jnp.concatenate([outputs, token_delta, scaled], axis=1)
    back = swap(back.reshape(experts, capacity, back.shape[1]), "exp").reshape(total, -1)

    down_grad = mm(hidden, out_delta, TN).astype(BF)
    gate_grad = mm(inputs, gate_delta, TN).astype(BF)
    up_grad = mm(inputs, up_delta, TN).astype(BF)

    mixed, token_grad, router_grad = pl.pallas_call(
        functools.partial(combine_kernel, capacity),
        out_shape=(
            jax.ShapeDtypeStruct((rows, width), BF),
            jax.ShapeDtypeStruct((rows, width), BF),
            jax.ShapeDtypeStruct((top, rows), BF),
        ),
        name="combine",
        in_specs=[pl.BlockSpec(memory_space=pltpu.VMEM)] * 5,
        out_specs=(pl.BlockSpec(memory_space=pltpu.VMEM),) * 3,
        compiler_params=pltpu.CompilerParams(vmem_limit_bytes=6 * 1024 * 1024),
    )(ids, weight, placing, weighting, back)
    router_grad = router_grad.T
    return (mixed, token_grad, router_grad, gate_grad[None], up_grad[None], down_grad[None])


def solution(mesh):
    return jax.shard_map(
        local,
        mesh=mesh,
        in_specs=(
            P("exp", "rep"),
            P("exp", "rep"),
            P("exp", None),
            P("exp", None),
            P("exp", "rep", None),
            P("exp", "rep", None),
            P("exp", None, "rep"),
        ),
        out_specs=(
            P("exp", "rep"),
            P("exp", "rep"),
            P("exp", None),
            P("exp", "rep", None),
            P("exp", "rep", None),
            P("exp", None, "rep"),
        ),
        check_vma=False,
    )
```

```python
import functools

import jax
import jax.numpy as jnp
from jax import lax
from jax.experimental import pallas as pl
from jax.experimental.pallas import tpu as pltpu
from jax.sharding import PartitionSpec as P

BF = jnp.bfloat16
F32 = jnp.float32
LANES = 128


def mm(a, b, dims=(((1,), (0,)), ((), ()))):
    return lax.dot_general(a, b, dims, preferred_element_type=F32)


NT = (((1,), (1,)), ((), ()))
TN = (((0,), (0,)), ((), ()))


def swap(x, axis):
    return lax.all_to_all(x, axis, split_axis=0, concat_axis=0, tiled=True)


def place_kernel(
    capacity,
    ids_hbm,
    weight_hbm,
    tokens_hbm,
    cot_hbm,
    sent_ref,
    placing_ref,
    weighting_ref,
    ids_ref,
    weight_ref,
    tokens_ref,
    cot_ref,
    arrived,
):
    sources = (ids_hbm, weight_hbm, tokens_hbm, cot_hbm)
    buffers = (ids_ref, weight_ref, tokens_ref, cot_ref)
    copies = [
        pltpu.make_async_copy(source, buffer, arrived.at[i])
        for i, (source, buffer) in enumerate(zip(sources, buffers))
    ]
    for copy in copies:
        copy.start()
    copies[0].wait()
    copies[1].wait()
    top, rows = ids_ref.shape
    experts = sent_ref.shape[0]
    total = experts * capacity
    width = sent_ref.shape[2] // 2
    slot = lax.broadcasted_iota(jnp.int32, (total, rows), 0)
    expert = slot // capacity
    named = jnp.zeros((total, rows), F32)
    share = jnp.zeros((total, rows), F32)
    for k in range(top):
        hit = ids_ref[k : k + 1, :] == expert
        named = named + jnp.where(hit, 1.0, 0.0)
        share = share + jnp.where(hit, weight_ref[k : k + 1, :].astype(F32), 0.0)
    first = lax.broadcasted_iota(jnp.int32, (rows, rows), 0)
    second = lax.broadcasted_iota(jnp.int32, (rows, rows), 1)
    before = jnp.where(first < second, 1.0, 0.0).astype(BF)
    earlier = mm(named.astype(BF), before)
    here = (named > 0.0) & (earlier == (slot % capacity).astype(F32))
    placing = jnp.where(here, 1.0, 0.0).astype(BF)
    weighting = jnp.where(here, share, 0.0).astype(BF)
    placing_ref[...] = placing
    weighting_ref[...] = weighting
    shape = (experts, capacity, width)
    copies[2].wait()
    sent_ref[:, :, :width] = mm(placing, tokens_ref[...]).astype(BF).reshape(shape)
    copies[3].wait()
    sent_ref[:, :, width:] = mm(weighting, cot_ref[...]).astype(BF).reshape(shape)


def activate_kernel(pieces_ref, mine_ref):
    reps, part, triple = pieces_ref.shape
    hid = triple // 3

    def summed(i):
        terms = [pieces_ref[r, :, i * hid : (i + 1) * hid].astype(F32) for r in range(reps)]
        return functools.reduce(lambda a, b: a + b, terms)

    gate, upval, hidden_delta = summed(0), summed(1), summed(2)
    sigmoid = 1.0 / (1.0 + jnp.exp(-gate))
    active = gate * sigmoid
    hidden = (active * upval).astype(BF)
    gate_delta = (hidden_delta * upval * sigmoid * (1.0 + gate * (1.0 - sigmoid))).astype(BF)
    up_delta = (hidden_delta * active).astype(BF)
    scaled = jnp.sum(hidden.astype(F32) * hidden_delta, axis=1, keepdims=True)
    scaled = jnp.broadcast_to(scaled, (part, LANES)).astype(BF)
    for r in range(reps):
        mine_ref[r, :, :hid] = hidden
        mine_ref[r, :, hid : 2 * hid] = gate_delta
        mine_ref[r, :, 2 * hid : 3 * hid] = up_delta
        mine_ref[r, :, 3 * hid :] = scaled


def expand_kernel(full_ref, gate_ref, up_ref, down_ref, back_hbm, back_ref, leaving):
    hid, width = down_ref.shape
    capacity = back_ref.shape[1]
    chunks = leaving.shape[0]
    rows = full_ref.shape[0] // chunks
    copies = []
    for i in range(chunks):
        full = full_ref[i * rows : (i + 1) * rows, :]
        outputs = mm(full[:, :hid], down_ref[...]).astype(BF)
        token_delta = mm(full[:, hid : 2 * hid], gate_ref[...], NT)
        token_delta = (token_delta + mm(full[:, 2 * hid : 3 * hid], up_ref[...], NT)).astype(BF)
        mine = pl.ds(i * rows // capacity, rows // capacity)
        shape = (rows // capacity, capacity, width)
        back_ref[mine, :, :width] = outputs.reshape(shape)
        back_ref[mine, :, width : 2 * width] = token_delta.reshape(shape)
        back_ref[mine, :, 2 * width :] = full[:, 3 * hid :].reshape(shape[:2] + (LANES,))
        copy = pltpu.make_async_copy(back_ref.at[mine], back_hbm.at[mine], leaving.at[i])
        copy.start()
        copies.append(copy)
    for copy in copies:
        copy.wait()


def combine_kernel(
    capacity, ids_ref, weight_ref, placing_ref, weighting_ref, back_ref, mixed_ref, grad_ref, router_ref
):
    top, rows = ids_ref.shape
    total = placing_ref.shape[0]
    width = mixed_ref.shape[1]
    back = back_ref[...].reshape(total, back_ref.shape[2])
    mixed_ref[...] = mm(weighting_ref[...], back[:, :width], TN).astype(BF)
    grad_ref[...] = mm(placing_ref[...], back[:, width : 2 * width], TN).astype(BF)
    expert = lax.broadcasted_iota(jnp.int32, (total, rows), 0) // capacity
    routed = back[:, 2 * width :].astype(F32)[:, :rows] * placing_ref[...].astype(F32)
    sums = [
        jnp.sum(jnp.where(ids_ref[k : k + 1, :] == expert, routed, 0.0), axis=0, keepdims=True)
        for k in range(top)
    ]
    sums = jnp.concatenate(sums, axis=0) / weight_ref[...].astype(F32)
    router_ref[...] = sums.astype(BF)


def local(tokens, cotangent, router_weight, expert_ids, w_gate, w_up, w_down):
    experts = lax.axis_size("exp")
    reps = lax.axis_size("rep")
    rows, top = expert_ids.shape
    capacity = min(rows, max(2, rows * top * 3 // (2 * experts)))
    width = tokens.shape[1]
    hid = w_gate.shape[2]
    total = experts * capacity
    part = total // reps
    gate_mat, up_mat, down_mat = w_gate[0], w_up[0], w_down[0]

    ids, weight = expert_ids.T, router_weight.T
    sent, placing, weighting = pl.pallas_call(
        functools.partial(place_kernel, capacity),
        out_shape=(
            jax.ShapeDtypeStruct((experts, capacity, 2 * width), BF),
            jax.ShapeDtypeStruct((total, rows), BF),
            jax.ShapeDtypeStruct((total, rows), BF),
        ),
        name="place",
        in_specs=[pl.BlockSpec(memory_space=pltpu.HBM)] * 4,
        out_specs=(pl.BlockSpec(memory_space=pltpu.VMEM),) * 3,
        scratch_shapes=[
            pltpu.VMEM((top, rows), jnp.int32),
            pltpu.VMEM((top, rows), BF),
            pltpu.VMEM((rows, width), BF),
            pltpu.VMEM((rows, width), BF),
            pltpu.SemaphoreType.DMA((4,)),
        ],
        compiler_params=pltpu.CompilerParams(vmem_limit_bytes=6 * 1024 * 1024),
    )(*(pltpu.with_memory_space_constraint(a, pltpu.HBM) for a in (ids, weight, tokens, cotangent)))
    recv = swap(sent, "exp").reshape(total, 2 * width)
    inputs, out_delta = recv[:, :width], recv[:, width:]

    partial = jnp.concatenate(
        [
            mm(inputs, gate_mat).astype(BF),
            mm(inputs, up_mat).astype(BF),
            mm(out_delta, down_mat, NT).astype(BF),
        ],
        axis=1,
    )
    pieces = swap(partial.reshape(reps, part, 3 * hid), "rep")
    mine = pl.pallas_call(
        activate_kernel,
        out_shape=jax.ShapeDtypeStruct((reps, part, 3 * hid + LANES), BF),
        name="activate",
        in_specs=[pl.BlockSpec(memory_space=pltpu.VMEM)],
        out_specs=pl.BlockSpec(memory_space=pltpu.VMEM),
        compiler_params=pltpu.CompilerParams(vmem_limit_bytes=8 * 1024 * 1024),
    )(pieces)
    full = swap(mine, "rep").reshape(total, -1)
    hidden, gate_delta = full[:, :hid], full[:, hid : 2 * hid]
    up_delta = full[:, 2 * hid : 3 * hid]

    shape = (experts, capacity, 2 * width + LANES)
    back = pl.pallas_call(
        expand_kernel,
        out_shape=jax.ShapeDtypeStruct(shape, BF),
        name="expand",
        in_specs=[pl.BlockSpec(memory_space=pltpu.VMEM)] * 4,
        out_specs=pl.BlockSpec(memory_space=pltpu.HBM),
        scratch_shapes=[pltpu.VMEM(shape, BF), pltpu.SemaphoreType.DMA((2,))],
        compiler_params=pltpu.CompilerParams(vmem_limit_bytes=12 * 1024 * 1024),
    )(full, gate_mat, up_mat, down_mat)
    back = swap(back, "exp")

    down_grad = mm(hidden, out_delta, TN).astype(BF)
    gate_grad = mm(inputs, gate_delta, TN).astype(BF)
    up_grad = mm(inputs, up_delta, TN).astype(BF)

    mixed, token_grad, router_grad = pl.pallas_call(
        functools.partial(combine_kernel, capacity),
        out_shape=(
            jax.ShapeDtypeStruct((rows, width), BF),
            jax.ShapeDtypeStruct((rows, width), BF),
            jax.ShapeDtypeStruct((top, rows), BF),
        ),
        name="combine",
        in_specs=[pl.BlockSpec(memory_space=pltpu.VMEM)] * 5,
        out_specs=(pl.BlockSpec(memory_space=pltpu.VMEM),) * 3,
        compiler_params=pltpu.CompilerParams(vmem_limit_bytes=6 * 1024 * 1024),
    )(ids, weight, placing, weighting, back)
    router_grad = router_grad.T
    return (mixed, token_grad, router_grad, gate_grad[None], up_grad[None], down_grad[None])


def solution(mesh):
    return jax.shard_map(
        local,
        mesh=mesh,
        in_specs=(
            P("exp", "rep"),
            P("exp", "rep"),
            P("exp", None),
            P("exp", None),
            P("exp", "rep", None),
            P("exp", "rep", None),
            P("exp", None, "rep"),
        ),
        out_specs=(
            P("exp", "rep"),
            P("exp", "rep"),
            P("exp", None),
            P("exp", "rep", None),
            P("exp", "rep", None),
            P("exp", None, "rep"),
        ),
        check_vma=False,
    )
```

```python
import functools

import jax
import jax.numpy as jnp
from jax import lax
from jax.experimental import pallas as pl
from jax.experimental.pallas import tpu as pltpu
from jax.sharding import PartitionSpec as P

BF = jnp.bfloat16
F32 = jnp.float32
LANES = 128


def mm(a, b, dims=(((1,), (0,)), ((), ()))):
    return lax.dot_general(a, b, dims, preferred_element_type=F32)


NT = (((1,), (1,)), ((), ()))
TN = (((0,), (0,)), ((), ()))


def swap(x, axis):
    return lax.all_to_all(x, axis, split_axis=0, concat_axis=0, tiled=True)


def place_kernel(
    capacity,
    ids_hbm,
    weight_hbm,
    tokens_hbm,
    cot_hbm,
    gate_hbm,
    up_hbm,
    down_hbm,
    sent_ref,
    placing_ref,
    weighting_ref,
    gate_ref,
    up_ref,
    down_ref,
    ids_ref,
    weight_ref,
    tokens_ref,
    cot_ref,
    arrived,
):
    sources = (ids_hbm, weight_hbm, tokens_hbm, cot_hbm, gate_hbm, up_hbm, down_hbm)
    buffers = (ids_ref, weight_ref, tokens_ref, cot_ref, gate_ref, up_ref, down_ref)
    copies = [
        pltpu.make_async_copy(source, buffer, arrived.at[i])
        for i, (source, buffer) in enumerate(zip(sources, buffers))
    ]
    for copy in copies:
        copy.start()
    copies[0].wait()
    copies[1].wait()
    top, rows = ids_ref.shape
    experts = sent_ref.shape[0]
    total = experts * capacity
    width = sent_ref.shape[2] // 2
    slot = lax.broadcasted_iota(jnp.int32, (total, rows), 0)
    expert = slot // capacity
    named = jnp.zeros((total, rows), F32)
    share = jnp.zeros((total, rows), F32)
    for k in range(top):
        hit = ids_ref[k : k + 1, :] == expert
        named = named + jnp.where(hit, 1.0, 0.0)
        share = share + jnp.where(hit, weight_ref[k : k + 1, :].astype(F32), 0.0)
    first = lax.broadcasted_iota(jnp.int32, (rows, rows), 0)
    second = lax.broadcasted_iota(jnp.int32, (rows, rows), 1)
    before = jnp.where(first < second, 1.0, 0.0).astype(BF)
    earlier = mm(named.astype(BF), before)
    here = (named > 0.0) & (earlier == (slot % capacity).astype(F32))
    placing = jnp.where(here, 1.0, 0.0).astype(BF)
    weighting = jnp.where(here, share, 0.0).astype(BF)
    placing_ref[...] = placing
    weighting_ref[...] = weighting
    shape = (experts, capacity, width)
    copies[2].wait()
    sent_ref[:, :, :width] = mm(placing, tokens_ref[...]).astype(BF).reshape(shape)
    copies[3].wait()
    sent_ref[:, :, width:] = mm(weighting, cot_ref[...]).astype(BF).reshape(shape)
    for copy in copies[4:]:
        copy.wait()


def partial_kernel(recv_ref, gate_ref, up_ref, down_ref, out_ref):
    experts, capacity, both = recv_ref.shape
    hid = gate_ref.shape[1]
    shape = (experts * capacity, both // 2)
    inputs = recv_ref[:, :, : both // 2].reshape(shape)
    out_delta = recv_ref[:, :, both // 2 :].reshape(shape)
    out_ref[:, :hid] = mm(inputs, gate_ref[...]).astype(BF)
    out_ref[:, hid : 2 * hid] = mm(inputs, up_ref[...]).astype(BF)
    out_ref[:, 2 * hid :] = mm(out_delta, down_ref[...], NT).astype(BF)


def activate_kernel(pieces_ref, mine_ref):
    reps, part, triple = pieces_ref.shape
    hid = triple // 3

    def summed(i):
        terms = [pieces_ref[r, :, i * hid : (i + 1) * hid].astype(F32) for r in range(reps)]
        return functools.reduce(lambda a, b: a + b, terms)

    gate, upval, hidden_delta = summed(0), summed(1), summed(2)
    sigmoid = 1.0 / (1.0 + jnp.exp(-gate))
    active = gate * sigmoid
    hidden = (active * upval).astype(BF)
    gate_delta = (hidden_delta * upval * sigmoid * (1.0 + gate * (1.0 - sigmoid))).astype(BF)
    up_delta = (hidden_delta * active).astype(BF)
    scaled = jnp.sum(hidden.astype(F32) * hidden_delta, axis=1, keepdims=True)
    scaled = jnp.broadcast_to(scaled, (part, LANES)).astype(BF)
    for r in range(reps):
        mine_ref[r, :, :hid] = hidden
        mine_ref[r, :, hid : 2 * hid] = gate_delta
        mine_ref[r, :, 2 * hid : 3 * hid] = up_delta
        mine_ref[r, :, 3 * hid :] = scaled


def expand_kernel(full_ref, gate_ref, up_ref, down_ref, back_hbm, back_ref, leaving):
    hid, width = down_ref.shape
    experts, capacity, _ = back_ref.shape
    shape = (experts, capacity, width)

    def send(i, columns):
        copy = pltpu.make_async_copy(
            back_ref.at[:, :, columns], back_hbm.at[:, :, columns], leaving.at[i]
        )
        copy.start()
        return copy

    outputs = mm(full_ref[:, :hid], down_ref[...]).astype(BF)
    back_ref[:, :, :width] = outputs.reshape(shape)
    first = send(0, pl.ds(0, width))
    token_delta = mm(full_ref[:, hid : 2 * hid], gate_ref[...], NT)
    token_delta = token_delta + mm(full_ref[:, 2 * hid : 3 * hid], up_ref[...], NT)
    back_ref[:, :, width : 2 * width] = token_delta.astype(BF).reshape(shape)
    back_ref[:, :, 2 * width :] = full_ref[:, 3 * hid :].reshape(shape[:2] + (LANES,))
    second = send(1, pl.ds(width, width + LANES))
    first.wait()
    second.wait()


def combine_kernel(
    capacity, ids_ref, weight_ref, placing_ref, weighting_ref, back_ref, mixed_ref, grad_ref, router_ref
):
    top, rows = ids_ref.shape
    total = placing_ref.shape[0]
    width = mixed_ref.shape[1]
    back = back_ref[...].reshape(total, back_ref.shape[2])
    mixed_ref[...] = mm(weighting_ref[...], back[:, :width], TN).astype(BF)
    grad_ref[...] = mm(placing_ref[...], back[:, width : 2 * width], TN).astype(BF)
    expert = lax.broadcasted_iota(jnp.int32, (total, rows), 0) // capacity
    routed = back[:, 2 * width :].astype(F32)[:, :rows] * placing_ref[...].astype(F32)
    sums = [
        jnp.sum(jnp.where(ids_ref[k : k + 1, :] == expert, routed, 0.0), axis=0, keepdims=True)
        for k in range(top)
    ]
    sums = jnp.concatenate(sums, axis=0) / weight_ref[...].astype(F32)
    router_ref[...] = sums.astype(BF)


def local(tokens, cotangent, router_weight, expert_ids, w_gate, w_up, w_down):
    experts = lax.axis_size("exp")
    reps = lax.axis_size("rep")
    rows, top = expert_ids.shape
    capacity = min(rows, max(2, rows * top * 3 // (2 * experts)))
    width = tokens.shape[1]
    hid = w_gate.shape[2]
    total = experts * capacity
    part = total // reps

    ids, weight = expert_ids.T, router_weight.T
    sent, placing, weighting, gate_mat, up_mat, down_mat = pl.pallas_call(
        functools.partial(place_kernel, capacity),
        out_shape=(
            jax.ShapeDtypeStruct((experts, capacity, 2 * width), BF),
            jax.ShapeDtypeStruct((total, rows), BF),
            jax.ShapeDtypeStruct((total, rows), BF),
            jax.ShapeDtypeStruct(w_gate.shape[1:], BF),
            jax.ShapeDtypeStruct(w_up.shape[1:], BF),
            jax.ShapeDtypeStruct(w_down.shape[1:], BF),
        ),
        name="place",
        in_specs=[pl.BlockSpec(memory_space=pltpu.HBM)] * 7,
        out_specs=(pl.BlockSpec(memory_space=pltpu.VMEM),) * 6,
        scratch_shapes=[
            pltpu.VMEM((top, rows), jnp.int32),
            pltpu.VMEM((top, rows), BF),
            pltpu.VMEM((rows, width), BF),
            pltpu.VMEM((rows, width), BF),
            pltpu.SemaphoreType.DMA((7,)),
        ],
        compiler_params=pltpu.CompilerParams(vmem_limit_bytes=6 * 1024 * 1024),
    )(*(pltpu.with_memory_space_constraint(a, pltpu.HBM) for a in (ids, weight, tokens, cotangent, w_gate[0], w_up[0], w_down[0])))
    recv = swap(sent, "exp")
    partial = pl.pallas_call(
        partial_kernel,
        out_shape=jax.ShapeDtypeStruct((total, 3 * hid), BF),
        name="partial",
        in_specs=[pl.BlockSpec(memory_space=pltpu.VMEM)] * 4,
        out_specs=pl.BlockSpec(memory_space=pltpu.VMEM),
        compiler_params=pltpu.CompilerParams(vmem_limit_bytes=16 * 1024 * 1024),
    )(recv, gate_mat, up_mat, down_mat)
    recv = recv.reshape(total, 2 * width)
    inputs, out_delta = recv[:, :width], recv[:, width:]
    pieces = swap(partial.reshape(reps, part, 3 * hid), "rep")
    mine = pl.pallas_call(
        activate_kernel,
        out_shape=jax.ShapeDtypeStruct((reps, part, 3 * hid + LANES), BF),
        name="activate",
        in_specs=[pl.BlockSpec(memory_space=pltpu.VMEM)],
        out_specs=pl.BlockSpec(memory_space=pltpu.VMEM),
        compiler_params=pltpu.CompilerParams(vmem_limit_bytes=8 * 1024 * 1024),
    )(pieces)
    full = swap(mine, "rep").reshape(total, -1)
    hidden, gate_delta = full[:, :hid], full[:, hid : 2 * hid]
    up_delta = full[:, 2 * hid : 3 * hid]

    shape = (experts, capacity, 2 * width + LANES)
    back = pl.pallas_call(
        expand_kernel,
        out_shape=jax.ShapeDtypeStruct(shape, BF),
        name="expand",
        in_specs=[pl.BlockSpec(memory_space=pltpu.VMEM)] * 4,
        out_specs=pl.BlockSpec(memory_space=pltpu.HBM),
        scratch_shapes=[pltpu.VMEM(shape, BF), pltpu.SemaphoreType.DMA((2,))],
        compiler_params=pltpu.CompilerParams(vmem_limit_bytes=12 * 1024 * 1024),
    )(full, gate_mat, up_mat, down_mat)
    back = swap(back, "exp")

    down_grad = mm(hidden, out_delta, TN).astype(BF)
    gate_grad = mm(inputs, gate_delta, TN).astype(BF)
    up_grad = mm(inputs, up_delta, TN).astype(BF)

    mixed, token_grad, router_grad = pl.pallas_call(
        functools.partial(combine_kernel, capacity),
        out_shape=(
            jax.ShapeDtypeStruct((rows, width), BF),
            jax.ShapeDtypeStruct((rows, width), BF),
            jax.ShapeDtypeStruct((top, rows), BF),
        ),
        name="combine",
        in_specs=[pl.BlockSpec(memory_space=pltpu.VMEM)] * 5,
        out_specs=(pl.BlockSpec(memory_space=pltpu.VMEM),) * 3,
        compiler_params=pltpu.CompilerParams(vmem_limit_bytes=6 * 1024 * 1024),
    )(ids, weight, placing, weighting, back)
    router_grad = router_grad.T
    return (mixed, token_grad, router_grad, gate_grad[None], up_grad[None], down_grad[None])


def solution(mesh):
    return jax.shard_map(
        local,
        mesh=mesh,
        in_specs=(
            P("exp", "rep"),
            P("exp", "rep"),
            P("exp", None),
            P("exp", None),
            P("exp", "rep", None),
            P("exp", "rep", None),
            P("exp", None, "rep"),
        ),
        out_specs=(
            P("exp", "rep"),
            P("exp", "rep"),
            P("exp", None),
            P("exp", "rep", None),
            P("exp", "rep", None),
            P("exp", None, "rep"),
        ),
        check_vma=False,
    )
```

```python
import functools

import jax
import jax.numpy as jnp
from jax import lax
from jax.experimental import pallas as pl
from jax.experimental.pallas import tpu as pltpu
from jax.sharding import PartitionSpec as P

BF = jnp.bfloat16
F32 = jnp.float32
LANES = 128


def mm(a, b, dims=(((1,), (0,)), ((), ()))):
    return lax.dot_general(a, b, dims, preferred_element_type=F32)


NT = (((1,), (1,)), ((), ()))
TN = (((0,), (0,)), ((), ()))


def swap(x, axis):
    return lax.all_to_all(x, axis, split_axis=0, concat_axis=0, tiled=True)


def place_kernel(
    capacity,
    ids_hbm,
    weight_hbm,
    tokens_hbm,
    cot_hbm,
    gate_hbm,
    up_hbm,
    down_hbm,
    sent_ref,
    placing_ref,
    weighting_ref,
    gate_ref,
    up_ref,
    down_ref,
    ids_ref,
    weight_ref,
    tokens_ref,
    cot_ref,
    arrived,
):
    sources = (ids_hbm, weight_hbm, tokens_hbm, cot_hbm, gate_hbm, up_hbm, down_hbm)
    buffers = (ids_ref, weight_ref, tokens_ref, cot_ref, gate_ref, up_ref, down_ref)
    copies = [
        pltpu.make_async_copy(source, buffer, arrived.at[i])
        for i, (source, buffer) in enumerate(zip(sources, buffers))
    ]
    for copy in copies:
        copy.start()
    copies[0].wait()
    copies[1].wait()
    top, rows = ids_ref.shape
    experts = sent_ref.shape[0]
    total = experts * capacity
    width = sent_ref.shape[2] // 2
    slot = lax.broadcasted_iota(jnp.int32, (total, rows), 0)
    expert = slot // capacity
    named = jnp.zeros((total, rows), F32)
    share = jnp.zeros((total, rows), F32)
    for k in range(top):
        hit = ids_ref[k : k + 1, :] == expert
        named = named + jnp.where(hit, 1.0, 0.0)
        share = share + jnp.where(hit, weight_ref[k : k + 1, :].astype(F32), 0.0)
    first = lax.broadcasted_iota(jnp.int32, (rows, rows), 0)
    second = lax.broadcasted_iota(jnp.int32, (rows, rows), 1)
    before = jnp.where(first < second, 1.0, 0.0).astype(BF)
    earlier = mm(named.astype(BF), before)
    here = (named > 0.0) & (earlier == (slot % capacity).astype(F32))
    placing = jnp.where(here, 1.0, 0.0).astype(BF)
    weighting = jnp.where(here, share, 0.0).astype(BF)
    placing_ref[...] = placing
    weighting_ref[...] = weighting
    shape = (experts, capacity, width)
    copies[2].wait()
    sent_ref[:, :, :width] = mm(placing, tokens_ref[...]).astype(BF).reshape(shape)
    copies[3].wait()
    sent_ref[:, :, width:] = mm(weighting, cot_ref[...]).astype(BF).reshape(shape)
    for copy in copies[4:]:
        copy.wait()


def partial_kernel(recv_ref, gate_ref, up_ref, down_ref, out_ref):
    experts, capacity, both = recv_ref.shape
    hid = gate_ref.shape[1]
    shape = (experts * capacity, both // 2)
    inputs = recv_ref[:, :, : both // 2].reshape(shape)
    out_delta = recv_ref[:, :, both // 2 :].reshape(shape)
    out_ref[:, :hid] = mm(inputs, gate_ref[...]).astype(BF)
    out_ref[:, hid : 2 * hid] = mm(inputs, up_ref[...]).astype(BF)
    out_ref[:, 2 * hid :] = mm(out_delta, down_ref[...], NT).astype(BF)


def activate_kernel(pieces_ref, mine_ref):
    reps, part, triple = pieces_ref.shape
    hid = triple // 3

    def summed(i):
        terms = [pieces_ref[r, :, i * hid : (i + 1) * hid].astype(F32) for r in range(reps)]
        return functools.reduce(lambda a, b: a + b, terms)

    gate, upval, hidden_delta = summed(0), summed(1), summed(2)
    sigmoid = 1.0 / (1.0 + jnp.exp(-gate))
    active = gate * sigmoid
    hidden = (active * upval).astype(BF)
    gate_delta = (hidden_delta * upval * sigmoid * (1.0 + gate * (1.0 - sigmoid))).astype(BF)
    up_delta = (hidden_delta * active).astype(BF)
    scaled = jnp.sum(hidden.astype(F32) * hidden_delta, axis=1, keepdims=True)
    scaled = jnp.broadcast_to(scaled, (part, LANES)).astype(BF)
    for r in range(reps):
        mine_ref[r, :, :hid] = hidden
        mine_ref[r, :, hid : 2 * hid] = gate_delta
        mine_ref[r, :, 2 * hid : 3 * hid] = up_delta
        mine_ref[r, :, 3 * hid :] = scaled


def expand_kernel(full_ref, gate_ref, up_ref, down_ref, back_ref):
    hid, width = down_ref.shape
    experts, capacity, _ = back_ref.shape
    shape = (experts, capacity, width)
    outputs = mm(full_ref[:, :hid], down_ref[...]).astype(BF)
    back_ref[:, :, :width] = outputs.reshape(shape)
    token_delta = mm(full_ref[:, hid : 2 * hid], gate_ref[...], NT)
    token_delta = token_delta + mm(full_ref[:, 2 * hid : 3 * hid], up_ref[...], NT)
    back_ref[:, :, width : 2 * width] = token_delta.astype(BF).reshape(shape)
    back_ref[:, :, 2 * width :] = full_ref[:, 3 * hid :].reshape(shape[:2] + (LANES,))


def finish_kernel(
    capacity,
    ids_ref,
    weight_ref,
    placing_ref,
    weighting_ref,
    full_ref,
    recv_ref,
    back_ref,
    mixed_hbm,
    grad_hbm,
    router_hbm,
    gate_hbm,
    up_hbm,
    down_hbm,
    mixed_ref,
    grad_ref,
    router_ref,
    gate_ref,
    up_ref,
    down_ref,
    leaving,
):
    top, rows = ids_ref.shape
    total = placing_ref.shape[0]
    width = mixed_ref.shape[1]
    hid = gate_ref.shape[1]
    inputs = recv_ref[:, :, :width].reshape(total, width)
    out_delta = recv_ref[:, :, width:].reshape(total, width)
    copies = []

    def send(value, buffer, target):
        buffer[...] = value.astype(BF)
        copy = pltpu.make_async_copy(buffer, target, leaving.at[len(copies)])
        copy.start()
        copies.append(copy)

    send(mm(full_ref[:, :hid].T, out_delta), down_ref, down_hbm)
    inputs = inputs.T
    send(mm(inputs, full_ref[:, hid : 2 * hid]), gate_ref, gate_hbm)
    send(mm(inputs, full_ref[:, 2 * hid : 3 * hid]), up_ref, up_hbm)
    back = back_ref[...]
    send(mm(weighting_ref[...], back[:, :width], TN), mixed_ref, mixed_hbm)
    send(mm(placing_ref[...], back[:, width : 2 * width], TN), grad_ref, grad_hbm)
    expert = lax.broadcasted_iota(jnp.int32, (total, rows), 0) // capacity
    routed = back[:, 2 * width :].astype(F32)[:, :rows] * placing_ref[...].astype(F32)
    sums = [
        jnp.sum(jnp.where(ids_ref[k : k + 1, :] == expert, routed, 0.0), axis=0, keepdims=True)
        for k in range(top)
    ]
    sums = jnp.concatenate(sums, axis=0) / weight_ref[...].astype(F32)
    send(sums, router_ref, router_hbm)
    for copy in copies:
        copy.wait()


def local(tokens, cotangent, router_weight, expert_ids, w_gate, w_up, w_down):
    experts = lax.axis_size("exp")
    reps = lax.axis_size("rep")
    rows, top = expert_ids.shape
    capacity = min(rows, max(2, rows * top * 3 // (2 * experts)))
    width = tokens.shape[1]
    hid = w_gate.shape[2]
    total = experts * capacity
    part = total // reps

    ids, weight = expert_ids.T, router_weight.T
    sent, placing, weighting, gate_mat, up_mat, down_mat = pl.pallas_call(
        functools.partial(place_kernel, capacity),
        out_shape=(
            jax.ShapeDtypeStruct((experts, capacity, 2 * width), BF),
            jax.ShapeDtypeStruct((total, rows), BF),
            jax.ShapeDtypeStruct((total, rows), BF),
            jax.ShapeDtypeStruct(w_gate.shape[1:], BF),
            jax.ShapeDtypeStruct(w_up.shape[1:], BF),
            jax.ShapeDtypeStruct(w_down.shape[1:], BF),
        ),
        name="place",
        in_specs=[pl.BlockSpec(memory_space=pltpu.HBM)] * 7,
        out_specs=(pl.BlockSpec(memory_space=pltpu.VMEM),) * 6,
        scratch_shapes=[
            pltpu.VMEM((top, rows), jnp.int32),
            pltpu.VMEM((top, rows), BF),
            pltpu.VMEM((rows, width), BF),
            pltpu.VMEM((rows, width), BF),
            pltpu.SemaphoreType.DMA((7,)),
        ],
        compiler_params=pltpu.CompilerParams(vmem_limit_bytes=6 * 1024 * 1024),
    )(*(pltpu.with_memory_space_constraint(a, pltpu.HBM) for a in (ids, weight, tokens, cotangent, w_gate[0], w_up[0], w_down[0])))
    recv = swap(sent, "exp")
    partial = pl.pallas_call(
        partial_kernel,
        out_shape=jax.ShapeDtypeStruct((total, 3 * hid), BF),
        name="partial",
        in_specs=[pl.BlockSpec(memory_space=pltpu.VMEM)] * 4,
        out_specs=pl.BlockSpec(memory_space=pltpu.VMEM),
        compiler_params=pltpu.CompilerParams(vmem_limit_bytes=16 * 1024 * 1024),
    )(recv, gate_mat, up_mat, down_mat)
    pieces = swap(partial.reshape(reps, part, 3 * hid), "rep")
    mine = pl.pallas_call(
        activate_kernel,
        out_shape=jax.ShapeDtypeStruct((reps, part, 3 * hid + LANES), BF),
        name="activate",
        in_specs=[pl.BlockSpec(memory_space=pltpu.VMEM)],
        out_specs=pl.BlockSpec(memory_space=pltpu.VMEM),
        compiler_params=pltpu.CompilerParams(vmem_limit_bytes=8 * 1024 * 1024),
    )(pieces)
    full = swap(mine, "rep").reshape(total, -1)
    shape = (experts, capacity, 2 * width + LANES)
    back = pl.pallas_call(
        expand_kernel,
        out_shape=jax.ShapeDtypeStruct(shape, BF),
        name="expand",
        in_specs=[pl.BlockSpec(memory_space=pltpu.VMEM)] * 4,
        out_specs=pl.BlockSpec(memory_space=pltpu.VMEM),
        compiler_params=pltpu.CompilerParams(vmem_limit_bytes=12 * 1024 * 1024),
    )(full, gate_mat, up_mat, down_mat)
    back = swap(back, "exp")

    vmem, hbm = pl.BlockSpec(memory_space=pltpu.VMEM), pl.BlockSpec(memory_space=pltpu.HBM)
    grads = [(width, hid), (width, hid), (hid, width)]
    small = [(rows, width), (rows, width), (top, rows)]
    mixed, token_grad, router_grad, gate_grad, up_grad, down_grad = pl.pallas_call(
        functools.partial(finish_kernel, capacity),
        out_shape=(
            jax.ShapeDtypeStruct((rows, width), BF),
            jax.ShapeDtypeStruct((rows, width), BF),
            jax.ShapeDtypeStruct((top, rows), BF),
        )
        + tuple(jax.ShapeDtypeStruct(g, BF) for g in grads),
        name="finish",
        in_specs=[vmem] * 7,
        out_specs=(hbm,) * 6,
        scratch_shapes=[pltpu.VMEM(g, BF) for g in small + grads]
        + [pltpu.SemaphoreType.DMA((6,))],
        compiler_params=pltpu.CompilerParams(vmem_limit_bytes=24 * 1024 * 1024),
    )(ids, weight, placing, weighting, full, recv, back.reshape(total, -1))
    router_grad = router_grad.T
    return (mixed, token_grad, router_grad, gate_grad[None], up_grad[None], down_grad[None])


def solution(mesh):
    return jax.shard_map(
        local,
        mesh=mesh,
        in_specs=(
            P("exp", "rep"),
            P("exp", "rep"),
            P("exp", None),
            P("exp", None),
            P("exp", "rep", None),
            P("exp", "rep", None),
            P("exp", None, "rep"),
        ),
        out_specs=(
            P("exp", "rep"),
            P("exp", "rep"),
            P("exp", None),
            P("exp", "rep", None),
            P("exp", "rep", None),
            P("exp", None, "rep"),
        ),
        check_vma=False,
    )
```
